32 devices in a mesh: fsdp: 8 (over z, y), tp: 4 (over x, core).
Axes of the slice: x: 2, y: 2, z: 4, core: 2. Of those that a mesh axis runs over, the one named last changes fastest.
Arguments:
- states: bfloat16 [8, 8, 32, 4096], P('fsdp', None, None, 'tp'), may hold values from -40 to 40
- dest: int32 [8, 8], P('fsdp'), may hold values from 0 to 7, each once within a row
- lengths: int32 [8, 8], P('fsdp'), may hold values from 1 to 32, 160 in all within a row
- strata: int32 [8, 8, 1], P('fsdp'), may hold values from 0 to 7
- ffn_gain: float32 [4096], replicated, may hold values from 0.1 to 1.9
- gate_weight: bfloat16 [4096, 7168], P('fsdp', 'tp'), may hold values from -0.0703125 to 0.0703125
- up_weight: bfloat16 [4096, 7168], P('fsdp', 'tp'), may hold values from -0.1 to 0.1
- down_weight: bfloat16 [7168, 4096], P('tp', 'fsdp'), may hold values from -0.058238643 to 0.058238643
- final_gain: float32 [4096], replicated, may hold values from 0.1 to 1.9
- value_weight: float32 [4096], replicated, may hold values from -0.09375 to 0.09375
Outputs:
- rewards: float32 [8, 8], P('fsdp')
- stratum_means: float32 [8], replicated
The draws below stay inside these ranges and needn't reach their ends.
Inputs may be any that keep to these rules, and one draw needn't show every extreme that they name: Each row of dest is a permutation: every source group sends exactly one response to every scoring group. Each source group's lengths sum to 160. `strata`: every stratum holds at least one response.
All inputs are finite; a program needn't handle non-finite values.
Results may differ from the reference program's by a relative error of at most 0.004.
Values may be sent and summed in bfloat16 or wider, within the bound.
A program may use at most 128 MiB of HBM per device.

```python
import math
import jax
import jax.numpy as jnp
import numpy as np
from jax import lax

D = 4096
FF = 7168
LEN = 32
S = 8
GROUPS = 8
N_TP = 4


unit_groups = 8


def draw_states(key, part):
    first, second, third = jax.random.split(key, 3)
    shape = (GROUPS, GROUPS, LEN, D)
    base = jax.random.normal(first, shape, jnp.float32)
    lower, upper = (math.log(0.3), math.log(3.0))
    row_scale = jnp.exp(jax.random.uniform(second, (GROUPS, GROUPS, LEN, 1), jnp.float32, lower, upper))
    column_scale = jnp.exp(jax.random.uniform(third, (D,), jnp.float32, lower, upper))
    return jnp.clip(base * row_scale * column_scale, -40.0, 40.0).astype(jnp.bfloat16)


def unit_group_ids(key):
    return jax.random.randint(jax.random.fold_in(key, 101), (FF,), 0, unit_groups)


def group_coupling(key):
    magnitude = jax.random.uniform(jax.random.fold_in(key, 102), (unit_groups,), jnp.float32, 0.5, 0.9)
    signs = jax.random.randint(jax.random.fold_in(key, 103), (unit_groups,), 0, 2).astype(jnp.float32) * 2.0 - 1.0
    return magnitude * signs


def gate_matrix(key):
    noise = jnp.clip(jax.random.normal(jax.random.fold_in(key, 104), (D, FF), jnp.float32), -4.5, 4.5)
    return noise / math.sqrt(D)


def draw_gate_weight(key, part):
    return gate_matrix(key).astype(jnp.bfloat16)


def draw_up_weight(key, part):
    coupling = group_coupling(key)[unit_group_ids(key)]
    noise = jnp.clip(jax.random.normal(jax.random.fold_in(key, 105), (D, FF), jnp.float32), -4.5, 4.5) / math.sqrt(D)
    mixed = coupling[None, :] * gate_matrix(key) + jnp.sqrt(1.0 - coupling * coupling)[None, :] * noise
    return mixed.astype(jnp.bfloat16)


def draw_down_weight(key, part):
    noise = jnp.clip(jax.random.normal(jax.random.fold_in(key, 106), (FF, D), jnp.float32), -4.5, 4.5) / math.sqrt(FF)
    shared = jnp.clip(jax.random.normal(jax.random.fold_in(key, 107), (unit_groups, D), jnp.float32), -4.5, 4.5) * (6.0 / FF)
    return (noise + shared[unit_group_ids(key)]).astype(jnp.bfloat16)


def choose_distinct(rng, rows, amount, top, lift):
    ranking = jax.random.permutation(jax.random.fold_in(rng, 1), amount)
    boost = ranking
    for power in range(3):
        boost = boost * boost // amount
    boost = boost * lift // amount
    tickets = jax.random.randint(jax.random.fold_in(rng, 2), (rows, amount), 0, 4096) + boost
    fixed_rows = jax.random.permutation(jax.random.fold_in(rng, 3), rows)[jnp.arange(amount) % rows]
    tickets = jnp.where(jnp.arange(rows)[:, None] == fixed_rows[None, :], 1 << 14, tickets)
    merit = tickets * amount + jnp.arange(amount)
    return lax.top_k(merit.astype(jnp.int32), top)[1].astype(jnp.int32)


def length_profile(amount, total, most, skew):
    loads = [(1 << 20) // math.isqrt(grade ** skew) + 1 for grade in range(2, amount + 1)]
    surplus, holding = total - most - (amount - 1), [1] * (amount - 1)
    while surplus > 0:
        movable = [i for i in range(amount - 1) if holding[i] < most]
        mass, remaining = sum([loads[i] for i in movable]), surplus
        for i in movable:
            addition = min(most - holding[i], max(1, remaining * loads[i] // mass), surplus)
            holding[i] = holding[i] + addition
            surplus = surplus - addition
    return np.array([most] + holding)


def uneven(rng, amount, total, most, slope):
    if amount == 2:
        one = jax.random.randint(rng, (), max(1, total - most), min(most, total - 1) + 1)
        return jnp.stack([one, total - one])
    sizes = jnp.asarray(length_profile(amount, total, most, slope), jnp.int32)
    twos = (amount - 1) // 2
    donor, sink = sizes[1:1 + 2 * twos:2], sizes[2:2 + 2 * twos:2]
    margin = jnp.minimum(donor - 1, most - sink)
    moved = jax.random.randint(jax.random.fold_in(rng, 1), (twos,), 0, 1 << 20) % (margin + 1)
    sizes = sizes.at[1:1 + 2 * twos:2].set(donor - moved).at[2:2 + 2 * twos:2].set(sink + moved)
    return sizes[jax.random.permutation(jax.random.fold_in(rng, 2), amount)]


def gaussian(rng, dims, width, most, kind=jnp.bfloat16):
    result = width * jax.random.normal(rng, dims, jnp.float32)
    return jnp.clip(result, min=-most, max=most).astype(kind)


def setup_inputs(seed: int = 0) -> dict:
    key_list = jax.random.split(jax.random.key(seed), 11)
    return {
        "states": draw_states(jax.random.fold_in(key_list[10], 71), 0),
        "dest": jax.vmap(lambda own: jax.random.permutation(own, GROUPS))(jax.random.split(key_list[1], GROUPS)).reshape((GROUPS, GROUPS)).astype(jnp.int32),
        "lengths": jax.vmap(lambda own: uneven(own, GROUPS, GROUPS * LEN * 5 // 8, LEN, 2))(jax.random.split(key_list[2], GROUPS)).reshape((GROUPS, GROUPS)).astype(jnp.int32),
        "strata": choose_distinct(key_list[3], GROUPS * GROUPS, S, 1, 1024).reshape((GROUPS, GROUPS, 1)),
        "ffn_gain": jnp.clip(1.0 + 0.18 * jax.random.normal(key_list[4], (D,), jnp.float32), 0.1, 1.9),
        "gate_weight": draw_gate_weight(jax.random.fold_in(key_list[10], 71), 0),
        "up_weight": draw_up_weight(jax.random.fold_in(key_list[10], 71), 0),
        "down_weight": draw_down_weight(jax.random.fold_in(key_list[10], 71), 0),
        "final_gain": jnp.clip(1.0 + 0.18 * jax.random.normal(key_list[8], (D,), jnp.float32), 0.1, 1.9),
        "value_weight": gaussian(key_list[9], (D,), D ** -0.5, 0.09375, jnp.float32),
    }


epsilon = 1e-05

def score_group(group_states, group_len, ffn_gain, gate_weight, up_weight, down_weight, final_gain, value_weight):
    token_rows = group_states.reshape(-1, D)
    widened = token_rows.astype(jnp.float32)
    normed = (widened * lax.rsqrt(lax.optimization_barrier(jnp.mean(widened * widened, axis=1, keepdims=True)) + epsilon) * ffn_gain).astype(jnp.bfloat16)
    gate = jnp.dot(normed, gate_weight, preferred_element_type=jnp.float32)
    up_part = jnp.dot(normed, up_weight, preferred_element_type=jnp.float32)
    hidden = (jax.nn.silu(gate) * up_part).astype(jnp.bfloat16)
    block_width = FF // N_TP
    ffn_out = jnp.zeros(widened.shape, jnp.float32)
    for block_index in range(N_TP):
        lower = block_index * block_width
        partial_value = jnp.dot(hidden[:, lower:lower + block_width], down_weight[lower:lower + block_width], preferred_element_type=jnp.float32)
        rounded = lax.optimization_barrier(partial_value.astype(jnp.bfloat16))
        ffn_out = ffn_out + rounded.astype(jnp.float32)
    mixed = widened + ffn_out
    product = lax.optimization_barrier(jnp.sum(mixed * final_gain * value_weight, axis=1))
    value = product / jnp.sqrt(lax.optimization_barrier(jnp.mean(mixed * mixed, axis=1)) + epsilon)
    value = value.reshape(group_len.shape[0], LEN)
    positions = jnp.arange(LEN, dtype=jnp.int32)
    live_mask = (positions[None, :] < group_len[:, None]).astype(jnp.float32)
    return lax.optimization_barrier(jnp.sum(value * live_mask, axis=1)) / group_len.astype(jnp.float32)

def reference(states, dest, lengths, strata, ffn_gain, gate_weight, up_weight, down_weight, final_gain, value_weight):
    groups = dest.shape[0]
    slots = jnp.arange(groups, dtype=jnp.int32)
    picker = (dest[:, None, :] == slots[None, :, None]).astype(jnp.int32)
    source_slot = lax.optimization_barrier(jnp.sum(picker * slots[None, None, :], axis=2)).astype(jnp.int32)
    routed = jnp.take_along_axis(states, source_slot[:, :, None, None], axis=1)
    received = jnp.swapaxes(routed, 0, 1)
    recv_len = jnp.take_along_axis(lengths, source_slot, axis=1).T
    recv_str = jnp.take_along_axis(strata[:, :, 0], source_slot, axis=1).T

    def score(pair):
        return score_group(pair[0], pair[1], ffn_gain, gate_weight, up_weight, down_weight, final_gain, value_weight)
    rewards = lax.map(score, (received, recv_len))
    strata_ids = jnp.arange(S, dtype=jnp.int32)
    onehot = (recv_str[:, :, None] == strata_ids[None, None, :]).astype(jnp.float32)
    sums = lax.optimization_barrier(jnp.sum(rewards[:, :, None] * onehot, axis=(0, 1)))
    counts = lax.optimization_barrier(jnp.sum(onehot, axis=(0, 1)))
    return (rewards, sums / counts)
```

```python
import functools
import jax
import jax.numpy as jnp
from jax import lax
from jax.experimental import pallas as pl
from jax.experimental.pallas import tpu as pltpu
from jax.sharding import PartitionSpec as P

S = 8
epsilon = 1e-05
MESH = pl.DeviceIdType.MESH
F32 = jnp.float32
BF16 = jnp.bfloat16


def kernel(n, tp, inner, chunk, down_chunk, ahead, lag,
           packed, meta, ffn_gain, gate_w, up_w, down_w, final_gain, value_w, out,
           tok, scaled, gate_in, up_in, down_in, rs_send, rs_recv, hid, mix_send, mix_recv,
           sq_own, sq_recv, acc, stat_own, stat_recv, fin,
           tok_s, tok_r, w_s, w_r, d_s, d_r, rs_s, rs_r, h_s, h_r, m_s, m_r, q_s, q_r, st_s, st_r, f_s, f_r):
    live, width = packed.shape
    rows, units = gate_w.shape
    cols = down_w.shape[1]
    n_chunks = units // chunk
    n_down = cols // down_chunk
    f = lax.axis_index("fsdp")
    t = lax.axis_index("tp")
    o = f // inner
    i = f % inner

    def fs(outer, inn):
        return outer * inner + inn

    def remote(src, dst, ss, rs, dev):
        return pltpu.make_async_remote_copy(src_ref=src, dst_ref=dst, send_sem=ss, recv_sem=rs, device_id=dev, device_id_type=MESH)

    barrier = pltpu.get_barrier_semaphore()
    for r in range(1, n):
        pl.semaphore_signal(barrier, inc=1, device_id=((f + r) % n, t), device_id_type=MESH)
    for r in range(1, tp):
        pl.semaphore_signal(barrier, inc=1, device_id=(f, (t + r) % tp), device_id_type=MESH)
    for r in range(1, tp):
        pl.semaphore_signal(barrier, inc=1, device_id=(fs((o + r) % tp, i), o), device_id_type=MESH)

    @pl.when(o != t)
    def _():
        pl.semaphore_signal(barrier, inc=1, device_id=(f, o), device_id_type=MESH)

    diag = (o == t).astype(jnp.int32)
    pl.semaphore_wait(barrier, n - 1 + tp - 1 + tp - diag)

    def tok_copy(r):
        return remote(packed, tok.at[o], tok_s.at[r], tok_r.at[o], (fs(t, i), (t + r) % tp))

    def st_copy(r):
        return remote(stat_own, stat_recv.at[o], st_s.at[r], st_r.at[o], (fs(t, i), (t + r) % tp))

    for r in range(1, tp):
        tok_copy(r).start()

    @pl.when(o != t)
    def _():
        tok_copy(0).start()

    def w_copies(c):
        cs = pl.ds(c * chunk, chunk)
        found = []
        for r in range(1, inner):
            dev = (fs(o, (i + r) % inner), t)
            found.append(remote(gate_w.at[:, cs], gate_in.at[r - 1, :, cs], w_s.at[c, r - 1, 0], w_r.at[c, r - 1, 0], dev))
            found.append(remote(up_w.at[:, cs], up_in.at[r - 1, :, cs], w_s.at[c, r - 1, 1], w_r.at[c, r - 1, 1], dev))
        return found

    def d_copies(c):
        cs = pl.ds(c * down_chunk, down_chunk)
        return [remote(down_w.at[:, cs], down_in.at[r - 1, :, cs], d_s.at[c, r - 1], d_r.at[c, r - 1], (fs(o, (i + r) % inner), t))
                for r in range(1, inner)]

    stages = [functools.partial(w_copies, c) for c in range(n_chunks)] + [functools.partial(d_copies, c) for c in range(n_down)]

    def start_stage(k):
        if k < len(stages):
            for copy in stages[k]():
                copy.start()

    for k in range(ahead):
        start_stage(k)

    @pl.when(o == t)
    def _():
        tok[o] = packed[...]

    wide = packed[...].astype(F32)
    sq_own[...] = jnp.broadcast_to(jnp.sum(wide * wide, axis=1, keepdims=True), (live, 128))
    q_copies = [remote(sq_own, sq_recv.at[r - 1], q_s.at[r - 1], q_r.at[r - 1], (f, (t + r) % tp)) for r in range(1, tp)]
    for copy in q_copies:
        copy.start()

    mine = pl.ds(pl.multiple_of(o * width, width), width)
    gain = ffn_gain[:, mine]
    for q in range(tp):
        @pl.when((o != t) | (o != q))
        def _():
            remote(packed, tok.at[q], tok_s.at[0], tok_r.at[q], (f, t)).wait_recv()

        scaled[q * live:(q + 1) * live, :] = (tok[q].astype(F32) * gain).astype(BF16)

    for copy in q_copies:
        copy.wait_recv()
    squares = sq_own[:, :1]
    for r in range(1, tp):
        squares = squares + sq_recv[r - 1][:, :1]
    rstd = lax.rsqrt(squares / (width * tp) + epsilon)

    def rs_copies(c):
        return [remote(rs_send.at[c, (o + r) % tp], rs_recv.at[c, r - 1], rs_s.at[c, r - 1], rs_r.at[c, r - 1], (fs((o + r) % tp, i), t))
                for r in range(1, tp)]

    def h_copies(c):
        cs = pl.ds(c * chunk, chunk)
        return [remote(hid.at[o, :, cs], hid.at[o, :, cs], h_s.at[c, r - 1], h_r.at[c, r - 1], (fs((o + r) % tp, i), t))
                for r in range(1, tp)]

    def h_arrive(c):
        cs = pl.ds(c * chunk, chunk)
        for r in range(1, tp):
            src = (o - r + tp) % tp
            remote(hid.at[src, :, cs], hid.at[src, :, cs], h_s.at[c, r - 1], h_r.at[c, r - 1], (fs(src, i), t)).wait_recv()

    def x_block(r):
        k = (i - r + inner) % inner
        return scaled[:, pl.ds(pl.multiple_of(k * rows, rows), rows)]

    def finish(c):
        for copy in rs_copies(c):
            copy.wait_recv()
        both = rs_send[c, o].astype(F32)
        for r in range(1, tp):
            both = both + rs_recv[c, r - 1].astype(F32)
        both = both * rstd
        gate, up = both[:, :chunk], both[:, chunk:]
        hid[o, :, c * chunk:(c + 1) * chunk] = (gate / (1.0 + jnp.exp(-gate)) * up).astype(BF16)
        for copy in h_copies(c):
            copy.start()

    for c in range(n_chunks):
        for copy in w_copies(c):
            copy.wait_recv()
        start_stage(c + ahead)
        cs = slice(c * chunk, (c + 1) * chunk)
        for side, (own, arrived) in enumerate(((gate_w, gate_in), (up_w, up_in))):
            part = jnp.dot(x_block(0), own[:, cs], preferred_element_type=F32)
            for r in range(1, inner):
                part = part + jnp.dot(x_block(r), arrived[r - 1, :, cs], preferred_element_type=F32)
            rs_send[c, :, :, side * chunk:(side + 1) * chunk] = part.astype(BF16).reshape(tp, live, chunk)
        for copy in rs_copies(c):
            copy.start()
        if c >= lag:
            finish(c - lag)
    for c in range(n_chunks - lag, n_chunks):
        finish(c)
    for k in range(n_chunks + ahead, len(stages)):
        start_stage(k)
    for c in range(n_chunks):
        h_arrive(c)

    blocks = [(r, c) for r in range(inner) for c in range(n_down)]

    def m_copies(b):
        return [remote(mix_send.at[b, (t + r) % tp], mix_recv.at[b, r - 1], m_s.at[b, r - 1], m_r.at[b, r - 1], (f, (t + r) % tp))
                for r in range(1, tp)]

    acc[...] = jnp.zeros_like(acc)

    def mix(b):
        r, c = blocks[b]
        for copy in m_copies(b):
            copy.wait_recv()
        k = (i - r + inner) % inner
        at = pl.multiple_of(k * cols + c * down_chunk, 128)
        total = mix_send[b, t].astype(F32)
        for q in range(1, tp):
            total = total + mix_recv[b, q - 1].astype(F32)
        mixed = tok[t, :, pl.ds(at, down_chunk)].astype(F32) + total
        there = pl.ds(pl.multiple_of(o * width + at, 128), down_chunk)
        head = final_gain[:, there] * value_w[:, there]
        first, second = mixed * head, mixed * mixed
        for g in range(down_chunk // 128):
            lanes = slice(g * 128, (g + 1) * 128)
            acc[0, :live] += first[:, lanes]
            acc[1, :live] += second[:, lanes]

    for b, (r, c) in enumerate(blocks):
        cs = slice(c * down_chunk, (c + 1) * down_chunk)
        if r > 0:
            d_copies(c)[r - 1].wait_recv()
            weight = down_in[r - 1, :, cs]
        else:
            weight = down_w[:, cs]
        part = jnp.dot(hid[...].reshape(tp * live, units), weight, preferred_element_type=F32)
        mix_send[b] = part.astype(BF16).reshape(tp, live, down_chunk)
        for copy in m_copies(b):
            copy.start()
        if b >= 1:
            mix(b - 1)
    mix(len(blocks) - 1)

    ones = jnp.ones((8, 128), F32)
    for s in range(2):
        stat_own[s] = lax.dot_general(ones, acc[s], (((1,), (1,)), ((), ())), precision=lax.Precision.HIGHEST, preferred_element_type=F32)
    for r in range(1, tp):
        st_copy(r).start()

    @pl.when(o != t)
    def _():
        st_copy(0).start()

    @pl.when(o == t)
    def _():
        stat_recv[o] = stat_own[...]

    for q in range(tp):
        @pl.when((o != t) | (o != q))
        def _():
            remote(stat_own, stat_recv.at[q], st_s.at[0], st_r.at[q], (f, t)).wait_recv()

    totals = jnp.sum(stat_recv[...], axis=0)
    value = totals[0] * lax.rsqrt(totals[1] / (width * tp) + epsilon)
    begin, size, to, stratum = (meta[:, k:k + 1] for k in range(4))
    lane = lax.broadcasted_iota(jnp.int32, (n, value.shape[1]), 1)
    member = (lane >= begin) & (lane < begin + size)
    reward = jnp.sum(jnp.where(member, value[:1], 0.0), axis=1, keepdims=True) / size.astype(F32)
    lane = lax.broadcasted_iota(jnp.int32, (n, 128), 1)
    by_dest = jnp.sum(jnp.where(lane == to, reward, 0.0), axis=0, keepdims=True)
    sums = jnp.sum(jnp.where(lane == stratum, reward, 0.0), axis=0, keepdims=True)
    counts = jnp.sum(jnp.where(lane == stratum, 1.0, 0.0), axis=0, keepdims=True)
    row8 = lax.broadcasted_iota(jnp.int32, (8, 128), 0)
    lane8 = lax.broadcasted_iota(jnp.int32, (8, 128), 1)
    fin[f] = jnp.where(row8 == 0, by_dest, jnp.where(row8 == 1, sums, counts))
    f_copies = [remote(fin.at[f], fin.at[f], f_s.at[r - 1], f_r.at[r - 1], ((f + r) % n, t)) for r in range(1, n)]
    for copy in f_copies:
        copy.start()
    for r in range(1, n):
        src = (f - r + n) % n
        remote(fin.at[src], fin.at[src], f_s.at[r - 1], f_r.at[r - 1], (src, t)).wait_recv()
    grand = jnp.sum(fin[...], axis=0)
    means = grand[1:2] / jnp.where(lane8[:1] < S, grand[2:3], 1.0)
    final = jnp.where(row8 == 1, means, 0.0)
    for s in range(n):
        got = jnp.sum(jnp.where(lane8 == f, fin[s], 0.0), axis=1, keepdims=True)[:1]
        final = final + jnp.where((row8 == 0) & (lane8 == s), got, 0.0)
    out[...] = final

    for r in range(1, tp):
        tok_copy(r).wait_send()
        st_copy(r).wait_send()

    @pl.when(o != t)
    def _():
        tok_copy(0).wait_send()
        st_copy(0).wait_send()

    pending = q_copies + f_copies
    for stage in stages:
        pending += stage()
    for c in range(n_chunks):
        pending += rs_copies(c) + h_copies(c)
    for b in range(len(blocks)):
        pending += m_copies(b)
    for copy in pending:
        copy.wait_send()


def solution(mesh):
    n = mesh.shape["fsdp"]
    tp = mesh.shape["tp"]
    inner = n // tp

    def body(states, dest, lengths, strata, ffn_gain, gate_weight, up_weight, down_weight, final_gain, value_weight):
        groups, length, width = states.shape[1:]
        live = groups * length * 5 // 8
        rows, units = gate_weight.shape
        cols = down_weight.shape[1]
        chunk, down_chunk = 256, 256
        n_chunks, n_down = units // chunk, cols // down_chunk
        n_blocks = inner * n_down
        padded = -(-live // 128) * 128
        lens = lengths[0]
        slots = jnp.arange(groups, dtype=jnp.int32)
        starts = jnp.sum(jnp.where(slots[None, :] < slots[:, None], lens[None, :], 0), axis=1)
        positions = jnp.arange(length, dtype=jnp.int32)
        rank = jnp.where(positions[None, :] < lens[:, None], starts[:, None] + positions[None, :], -1).reshape(-1)
        pick = (rank[None, :] == jnp.arange(live, dtype=jnp.int32)[:, None]).astype(BF16)
        packed = jnp.dot(pick, states[0].reshape(groups * length, width), preferred_element_type=F32).astype(BF16)
        meta = jnp.stack([starts, lens, dest[0], strata[0, :, 0]], axis=1)
        vmem = pl.BlockSpec(memory_space=pltpu.VMEM)
        dma = pltpu.SemaphoreType.DMA
        out = pl.pallas_call(
            functools.partial(kernel, n, tp, inner, chunk, down_chunk, 2, 1),
            out_shape=jax.ShapeDtypeStruct((8, 128), F32),
            in_specs=[vmem] * 8,
            out_specs=vmem,
            scratch_shapes=[
                pltpu.VMEM((tp, live, width), BF16),
                pltpu.VMEM((tp * live, width), BF16),
                pltpu.VMEM((inner - 1, rows, units), BF16),
                pltpu.VMEM((inner - 1, rows, units), BF16),
                pltpu.VMEM((inner - 1, units, cols), BF16),
                pltpu.VMEM((n_chunks, tp, live, 2 * chunk), BF16),
                pltpu.VMEM((n_chunks, tp - 1, live, 2 * chunk), BF16),
                pltpu.VMEM((tp, live, units), BF16),
                pltpu.VMEM((n_blocks, tp, live, down_chunk), BF16),
                pltpu.VMEM((n_blocks, tp - 1, live, down_chunk), BF16),
                pltpu.VMEM((live, 128), F32),
                pltpu.VMEM((tp - 1, live, 128), F32),
                pltpu.VMEM((2, padded, 128), F32),
                pltpu.VMEM((2, 8, padded), F32),
                pltpu.VMEM((tp, 2, 8, padded), F32),
                pltpu.VMEM((n, 8, 128), F32),
                dma((tp,)), dma((tp,)),
                dma((n_chunks, inner - 1, 2)), dma((n_chunks, inner - 1, 2)),
                dma((n_down, inner - 1)), dma((n_down, inner - 1)),
                dma((n_chunks, tp - 1)), dma((n_chunks, tp - 1)),
                dma((n_chunks, tp - 1)), dma((n_chunks, tp - 1)),
                dma((n_blocks, tp - 1)), dma((n_blocks, tp - 1)),
                dma((tp - 1,)), dma((tp - 1,)),
                dma((tp,)), dma((tp,)),
                dma((n - 1,)), dma((n - 1,)),
            ],
            compiler_params=pltpu.CompilerParams(collective_id=0, has_side_effects=True, vmem_limit_bytes=62 << 20),
        )(packed, meta, ffn_gain[None], gate_weight, up_weight, down_weight, final_gain[None], value_weight[None])
        return out[:1, :groups], out[1, :S]

    return jax.shard_map(
        body,
        mesh=mesh,
        in_specs=(
            P("fsdp", None, None, "tp"),
            P("fsdp", None),
            P("fsdp", None),
            P("fsdp", None, None),
            P(),
            P("fsdp", "tp"),
            P("fsdp", "tp"),
            P("tp", "fsdp"),
            P(),
            P(),
        ),
        out_specs=(P("fsdp", None), P()),
        check_vma=False,
    )
```
